32 devices in a mesh: sub: 16 (over z, x, core), grid: 2 (over y).
Axes of the slice: x: 2, y: 2, z: 4, core: 2. Of those that a mesh axis runs over, the one named last changes fastest.
Arguments:
- front_entries: float32 [16, 12, 128, 2, 1536], P('sub', None, None, 'grid'), as said below
- coupling_rows: bfloat16 [16, 2048, 256], P('sub', 'grid'), may hold values from -0.09375 to 0.09375
- child_map: int32 [16, 2048], P('sub'), may hold values from 0 to 3071, as said below
Outputs:
- factored: float32 [16, 12, 128, 2, 1536], P('sub', None, None, 'grid')
The draws below stay inside these ranges and needn't reach their ends.
Inputs may be any that keep to these rules, and one draw needn't show every extreme that they name: `child_map`: rows 2 p and 2 p + 1 each hold 2048 distinct indices, and together they name every index of the parent front. `front_entries`: each front is symmetric, and stays positive definite after both children's updates are subtracted.
All inputs are finite; a program needn't handle non-finite values.
Results may differ from the reference program's by a relative error of at most 0.0003.
Values may be sent and summed in bfloat16 or wider, within the bound.
A program may use at most 128 MiB of HBM per device.

```python
import math
import jax
import jax.numpy as jnp
from jax import lax

NB = 128
PF = 3072
SEP = 2048
PIV = 1024
KL = 256
PARENTS = 8
RB = 12
CB = 12
N_SUB = 16
N_GRID = 2


def draw_front_entries(key, part):

    def one_parent(index):
        parent_key = jax.random.fold_in(key, index)
        noise_key, diag_key, sign_key, place_key, size_key = jax.random.split(parent_key, 5)
        spread = 1.6 / math.sqrt(PF)
        raw = spread * jax.random.truncated_normal(noise_key, -6.0, 6.0, (PF, PF), jnp.float32)
        diag = jax.random.uniform(diag_key, (PF,), jnp.float32, 8.0, 12.0)
        signs = 2.0 * jax.random.bernoulli(sign_key, 0.5, (PF,)).astype(jnp.float32) - 1.0
        weight = signs * jax.random.uniform(size_key, (PF,), jnp.float32, 0.5, 1.5)
        places = jax.random.uniform(place_key, (PF,), jnp.float32)
        smooth = 240.0 / PF * weight[:, None] * weight[None, :] * jnp.exp(-jnp.abs(places[:, None] - places[None, :]) / 0.3)
        symmetric = (raw + raw.T) * 0.7071067811865476
        identity = jnp.eye(PF, dtype=bool)
        whole = jnp.where(identity, diag[None, :], symmetric) + smooth
        return whole.reshape(RB, 2, NB, CB, N_GRID, NB).transpose(1, 0, 2, 4, 3, 5).reshape(2, RB, NB, N_GRID, CB * NB)
    output = lax.map(one_parent, jnp.arange(PARENTS, dtype=jnp.int32))
    return output.reshape(N_SUB, RB, NB, N_GRID, CB * NB)


def draw_child_map(key, part):

    def one_parent(index):
        order = jax.random.permutation(jax.random.fold_in(key, index + 7919), PF)
        return jnp.stack([order[:SEP], order[PF - SEP:]], 0)
    output = jax.vmap(one_parent)(jnp.arange(PARENTS, dtype=jnp.int32))
    return output.reshape(N_SUB, SEP).astype(jnp.int32)


def levels(key, dims, pieces, smallest, largest):
    factor_of, own = 1.0, jax.random.fold_in(key, 6)
    for axis_at, parts in pieces:
        draws = jnp.exp(jax.random.uniform(jax.random.fold_in(own, axis_at), (parts,), jnp.float32, smallest / len(pieces), largest / len(pieces)))
        factor_of = factor_of * jnp.repeat(draws, dims[axis_at] // parts).reshape([-1 if axis == axis_at else 1 for axis in range(len(dims))])
    return factor_of


def bell_draw(key, dims, scale, bound, cuts=(), held_as=jnp.bfloat16):
    drawn = scale * jax.random.normal(key, dims, jnp.float32)
    if cuts:
        drawn = drawn * levels(key, dims, cuts, -0.22, 0.18)
    return jnp.clip(drawn, -bound, bound).astype(held_as)


def setup_inputs(seed: int = 0) -> dict:
    seeds = jax.random.split(jax.random.key(seed), 4)
    front_entries = draw_front_entries(jax.random.fold_in(seeds[3], 71), 0)
    coupling_rows = bell_draw(seeds[1], (N_SUB, SEP, KL), (2 * (SEP + KL)) ** -0.5, 0.09375, ((0, 16), (1, 2)))
    child_map = draw_child_map(jax.random.fold_in(seeds[3], 71), 0)
    return dict(front_entries=front_entries, coupling_rows=coupling_rows, child_map=child_map)


def reference(front_entries, coupling_rows, child_map):
    fronts = front_entries.reshape(PARENTS, 2, RB, NB, N_GRID, CB * NB)
    factors = coupling_rows.reshape(PARENTS, 2, SEP, KL)
    mappings = child_map.reshape(PARENTS, 2, SEP)

    def one_parent(items):
        front, factor, mapping = items
        whole = front.reshape(2, RB, NB, N_GRID, CB, NB).transpose(1, 0, 2, 4, 3, 5).reshape(PF, PF)
        for child in range(2):
            update = jnp.dot(factor[child].astype(jnp.float32), factor[child].T.astype(jnp.float32), preferred_element_type=jnp.float32)
            whole = whole.at[mapping[child][:, None], mapping[child][None, :]].add(-update)
        pivot = jnp.tril(jnp.linalg.cholesky(whole[:PIV, :PIV]))
        below = jax.scipy.linalg.solve_triangular(pivot, whole[PIV:, :PIV].T, lower=True).T
        schur = whole[PIV:, PIV:] - jnp.dot(below, below.T, precision=lax.Precision.HIGHEST)
        result = jnp.zeros((PF, PF), jnp.float32)
        result = result.at[:PIV, :PIV].set(pivot).at[PIV:, :PIV].set(below).at[PIV:, PIV:].set(schur)
        return result.reshape(RB, 2, NB, CB, N_GRID, NB).transpose(1, 0, 2, 4, 3, 5).reshape(2, RB, NB, N_GRID, CB * NB)
    output = lax.map(one_parent, (fronts, factors, mappings))
    return output.reshape(N_SUB, RB, NB, N_GRID, CB * NB)
```

```python
import functools

import jax
import jax.numpy as jnp
from jax import lax
from jax.experimental import pallas as pl
from jax.experimental.pallas import tpu as pltpu
from jax.sharding import PartitionSpec as P

NB = 128
PF = 3072
PIV = 1024
NPB = PIV // NB
SUBL = 8
EXTRA = 16
NT = (((1,), (1,)), ((), ()))
NN = (((1,), (0,)), ((), ()))
F32 = jnp.float32
BF16 = jnp.bfloat16


def dot(a, b, dims=NN):
    return lax.dot_general(a, b, dims, preferred_element_type=F32)


def split(x):
    high = x.astype(BF16)
    return high, (x - high.astype(F32)).astype(BF16)


def dot3(a, b, dims=NN):
    ah, al = split(a)
    bh, bl = split(b)
    return dot(ah, bh, dims) + (dot(al, bh, dims) + dot(ah, bl, dims))


def sibling_swap(shard):
    return lax.ppermute(shard, "sub", [(i, i ^ 1) for i in range(lax.axis_size("sub"))])


def ring_gather(shard):
    count = lax.axis_size("grid")
    parts = [shard]
    for k in range(1, count):
        parts.append(lax.ppermute(shard, "grid", [((i + k) % count, i) for i in range(count)]))
    return jnp.stack(parts)


def block(index):
    return pl.ds(pl.multiple_of(index * NB, NB), NB)


def expand_kernel(map_ref, rows_ref, out_ref):
    rows = out_ref.shape[0]
    width = rows_ref.shape[2]
    first = pl.program_id(0) * rows
    for child in range(2):
        ids = first + lax.broadcasted_iota(jnp.int32, (rows, map_ref.shape[2]), 0)
        hot = jnp.where(map_ref[child] == ids, 1.0, 0.0).astype(BF16)
        out_ref[:, child * width : (child + 1) * width] = dot(hot, rows_ref[child]).astype(BF16)


def expand(maps, rows):
    tile = 256
    width = rows.shape[2]
    return pl.pallas_call(
        expand_kernel,
        grid=(PF // tile,),
        in_specs=[
            pl.BlockSpec(maps.shape, lambda i: (0, 0, 0)),
            pl.BlockSpec(rows.shape, lambda i: (0, 0, 0)),
        ],
        out_specs=pl.BlockSpec((tile, 2 * width), lambda i: (i, 0)),
        out_shape=jax.ShapeDtypeStruct((PF, 2 * width), BF16),
        name="expand",
    )(maps, rows)


def factor_block(diag):
    groups = NB // SUBL
    a = [diag[v * SUBL : (v + 1) * SUBL] for v in range(groups)]
    lane = lax.broadcasted_iota(jnp.int32, (SUBL, NB), 1)
    sub = lax.broadcasted_iota(jnp.int32, (SUBL, NB), 0)

    def along(x, row):
        return jnp.broadcast_to(x[row : row + 1], (SUBL, NB))

    for t in range(groups):
        cols = [
            [jnp.broadcast_to(a[v][:, t * SUBL + l : t * SUBL + l + 1], (SUBL, NB)) for l in range(SUBL)]
            for v in range(t, groups)
        ]
        for l in range(SUBL):
            inv_pivot = 1.0 / along(cols[0][l], l)
            row = along(a[t], l) * jnp.where(lane == t * SUBL + l, 2.0, 1.0)
            ahead = [along(cols[0][k], l) for k in range(l + 1, SUBL)]
            for v in range(t, groups):
                mine = cols[v - t]
                m = mine[l] * inv_pivot
                if v == t:
                    m = jnp.where(sub > l, m, 0.0)
                a[v] = a[v] - m * row
                for k in range(l + 1, SUBL):
                    mine[k] = mine[k] - m * ahead[k - l - 1]
    d_lane = jnp.zeros((SUBL, NB), F32)
    on_diag = []
    for v in range(groups):
        on_diag.append(jnp.where(lane == v * SUBL + sub, a[v], 0.0))
        d_lane = d_lane + on_diag[v]
    inv_lane = 1.0 / jnp.sum(d_lane, axis=0, keepdims=True)
    inverse, upper = [], []
    for v in range(groups):
        scale = 1.0 / jnp.sqrt(jnp.sum(on_diag[v], axis=1, keepdims=True))
        at = v * SUBL + sub
        inverse.append(jnp.where(lane <= at, a[v] * inv_lane * scale, 0.0))
        upper.append(jnp.where(lane >= at, a[v] * scale, 0.0))
    return jnp.concatenate(inverse, 0), jnp.concatenate(upper, 0)


def pivot_kernel(grid_count, me_ref, front_ref, rows_ref, factor_ref, high_ref, low_ref, w):
    s, g = me_ref[0], me_ref[1]
    held = front_ref.shape[2] - EXTRA
    eye = lax.broadcasted_iota(jnp.int32, (NB, NB), 0) == lax.broadcasted_iota(jnp.int32, (NB, NB), 1)
    for i in range(NPB):
        at = slice(i * NB, (i + 1) * NB)
        w[at, :] = -dot(rows_ref[at, :], rows_ref[...], NT)
        from_row = lax.rem(i + s, 2)
        for b in range(NPB):
            k = lax.rem(b - g + PIV // NB * grid_count, grid_count)
            cols = slice(b // grid_count * NB, (b // grid_count + 1) * NB)
            there = slice(b * NB, (b + 1) * NB)
            piece = front_ref[from_row, k, i // 2 * NB : (i // 2 + 1) * NB, cols].astype(F32)
            if b == i:
                rest = front_ref[from_row, k, held : held + EXTRA, cols].astype(F32)[:1]
                piece = piece + jnp.where(eye, rest, 0.0)
            w[at, there] += piece

    @pl.loop(0, NPB)
    def _(j):
        at = block(j)
        inverse, upper = factor_block(w[at, at])
        factor_ref[at, at] = upper.T
        w[at, at] = jnp.where(eye, 1.0, 0.0)
        panel = dot3(inverse, w[at, :])
        w[at, :] = panel
        panel16 = panel.astype(BF16)

        @pl.loop(j + 1, NPB)
        def _(i):
            mine = block(i)
            left = w[at, mine].T
            factor_ref[mine, at] = left
            w[mine, at] = jnp.zeros((NB, NB), F32)
            w[mine, :] -= dot(left.astype(BF16), panel16)

    for i in range(NPB):
        at = slice(i * NB, (i + 1) * NB)
        keep = lax.broadcasted_iota(jnp.int32, (NB, PIV), 1) < (i + 1) * NB
        high, low = split(jnp.where(keep, w[at, :], 0.0))
        high_ref[at, :] = high
        low_ref[at, :] = low


def factor_pivots(me, fronts, expanded, grid_count):
    vmem = pl.BlockSpec(memory_space=pltpu.VMEM)
    square = functools.partial(jax.ShapeDtypeStruct, (PIV, PIV))
    return pl.pallas_call(
        functools.partial(pivot_kernel, grid_count),
        grid=(1,),
        in_specs=[
            pl.BlockSpec(memory_space=pltpu.SMEM),
            vmem,
            pl.BlockSpec((PIV, expanded.shape[1]), lambda i: (0, 0)),
        ],
        out_specs=[vmem, vmem, vmem],
        out_shape=[square(F32), square(BF16), square(BF16)],
        scratch_shapes=[pltpu.VMEM((PIV, PIV), F32)],
        cost_estimate=pl.CostEstimate(flops=40 * PIV**3, bytes_accessed=16 * PIV**2, transcendentals=0),
        name="pivots",
    )(me, fronts, expanded)


def schur_kernel(
    grid_count, me_ref, front_ref, left_ref, right_ref, rows_ref, factor_ref, high_ref, low_ref,
    out_ref, mycols, across, xr, xl,
):
    s, g = me_ref[0], me_ref[1]
    r = pl.program_id(0)
    col_blocks = out_ref.shape[0] // NB
    done = NPB // grid_count

    @pl.when(r == 0)
    def _():
        for c in range(col_blocks):
            mycols[c * NB : (c + 1) * NB, :] = rows_ref[block(c * grid_count + g), :]
        for i in range(NPB):
            at = slice(i * NB, (i + 1) * NB)
            piece = right_ref[lax.rem(i + s, 2), i // 2 * NB : (i // 2 + 1) * NB, :].astype(F32)
            across[at, :] = (piece - dot(rows_ref[at, :], mycols[done * NB :, :], NT)).astype(BF16)
        for i in range(NPB):
            at = slice(i * NB, (i + 1) * NB)
            deep = (i + 1) * NB
            xr[at, :] = dot(high_ref[at, :deep], across[:deep, :]).astype(BF16)

    row_id = 2 * r + s

    @pl.when(r < NPB // 2)
    def _():
        for c in range(col_blocks):
            to = pl.ds(c, NB, stride=col_blocks)
            if c < done:
                col_id = c * grid_count + g
                here = factor_ref[block(row_id), block(col_id)]
                out_ref[to, :] = jnp.where(row_id >= col_id, here, 0.0)
            else:
                out_ref[to, :] = jnp.zeros((NB, NB), F32)

    @pl.when(r >= NPB // 2)
    def _():
        mine = rows_ref[block(row_id), :]
        local = block(r - NPB // 2)
        for b in range(NPB):
            k = lax.rem(b - g + NPB * grid_count, grid_count)
            cols = slice(b // grid_count * NB, (b // grid_count + 1) * NB)
            xl[:, b * NB : (b + 1) * NB] = left_ref[k, local, cols].astype(F32)
        a_high, a_low = split(xl[...] - dot(mine, rows_ref[:PIV, :], NT))
        x = dot(a_high, high_ref[...], NT) + (dot(a_low, high_ref[...], NT) + dot(a_high, low_ref[...], NT))
        xl[...] = x
        x16 = x.astype(BF16)
        taken = dot(mine, mycols[done * NB :, :], NT) + dot(x16, xr[...])
        for c in range(col_blocks):
            to = pl.ds(c, NB, stride=col_blocks)
            if c < done:
                out_ref[to, :] = xl[:, block(c * grid_count + g)]
            else:
                out_ref[to, :] = front_ref[to, :] - taken[:, (c - done) * NB : (c - done + 1) * NB]


def schur(me, front, left, right, expanded, factor, high, low, grid_count, col_blocks):
    vmem = pl.BlockSpec(memory_space=pltpu.VMEM)
    tall = NB * col_blocks
    below = (col_blocks - NPB // grid_count) * NB
    return pl.pallas_call(
        functools.partial(schur_kernel, grid_count),
        grid=(front.shape[0] // tall,),
        in_specs=[
            pl.BlockSpec(memory_space=pltpu.SMEM),
            pl.BlockSpec((tall, NB), lambda i: (jnp.maximum(i, NPB // 2), 0)),
        ]
        + [vmem] * 6,
        out_specs=pl.BlockSpec((tall, NB), lambda i: (i, 0)),
        out_shape=jax.ShapeDtypeStruct(front.shape, F32),
        scratch_shapes=[
            pltpu.VMEM((col_blocks * NB, expanded.shape[1]), BF16),
            pltpu.VMEM((PIV, below), BF16),
            pltpu.VMEM((PIV, below), BF16),
            pltpu.VMEM((NB, PIV), F32),
        ],
        compiler_params=pltpu.CompilerParams(vmem_limit_bytes=56 * 1024 * 1024),
        name="schur",
    )(me, front, left, right, expanded, factor, high, low)


def on_device(front_entries, coupling_rows, child_map):
    s = lax.axis_index("sub") % 2
    g = lax.axis_index("grid")
    grid_count = lax.axis_size("grid")
    row_blocks = front_entries.shape[1]
    col_width = front_entries.shape[4]
    col_blocks = col_width // NB
    wide = front_entries.reshape(row_blocks * NB, col_width)
    front = front_entries.reshape(row_blocks * NB * col_blocks, NB)
    me = jnp.stack([s, g]).astype(jnp.int32)
    top, pivot_cols = PIV // 2, PIV // grid_count

    own_rows = ring_gather(coupling_rows[0]).reshape(-1, coupling_rows.shape[2])
    own_map = jnp.roll(child_map[0].reshape(grid_count, -1), -g, axis=0).reshape(1, -1)
    rows = jnp.stack([own_rows, sibling_swap(own_rows)])
    maps = jnp.stack([own_map, sibling_swap(own_map)])

    corner = wide[:top, :pivot_cols]
    rounded = lax.reduce_precision(corner, 8, 7)
    row_ids = (jnp.arange(top, dtype=jnp.int32) // NB * 2 + s) * NB + jnp.arange(top, dtype=jnp.int32) % NB
    spots = jnp.arange(pivot_cols, dtype=jnp.int32)
    col_ids = (spots // NB * grid_count + g) * NB + spots % NB
    rest = jnp.sum(jnp.where(row_ids[:, None] == col_ids[None, :], corner - rounded, 0.0), axis=0)
    piece = jnp.concatenate(
        [corner.astype(BF16), jnp.broadcast_to(rest.astype(BF16)[None], (EXTRA, pivot_cols))]
    )
    held = ring_gather(piece)
    pivots = jnp.stack([held, sibling_swap(held)])
    left = ring_gather(wide[top:, :pivot_cols].astype(BF16))
    over = wide[:top, pivot_cols:].astype(BF16)
    right = jnp.stack([over, sibling_swap(over)])

    expanded = expand(maps, rows)
    factor, high, low = factor_pivots(me, pivots, expanded, grid_count)
    result = schur(me, front, left, right, expanded, factor, high, low, grid_count, col_blocks)
    return result.reshape(front_entries.shape)


def solution(mesh):
    return jax.shard_map(
        on_device,
        mesh=mesh,
        in_specs=(P("sub", None, None, "grid", None), P("sub", "grid", None), P("sub", None)),
        out_specs=P("sub", None, None, "grid", None),
        check_vma=False,
    )
```
